32 devices in a mesh: head: 4 (over x, core), blk: 8 (over z, y).
Axes of the slice: x: 2, y: 2, z: 4, core: 2. Of those that a mesh axis runs over, the one named last changes fastest.
Arguments:
- tokens: bfloat16 [8, 1024, 768], P('head', 'blk'), may hold values from -6 to 6
- lengths: int32 [8], replicated, may hold values from 256 to 1024, as said below
- slot_sequence: int32 [8], replicated, may hold values from 0 to 7, each once
- cotangent: bfloat16 [8, 1024, 768], P('head', 'blk'), may hold values from -6 to 6
- w_query: bfloat16 [2, 768, 768], P(None, ('head', 'blk')), may hold values from -0.3125 to 0.3125
- w_key: bfloat16 [2, 768, 768], P(None, ('head', 'blk')), may hold values from -0.3125 to 0.3125
- w_value: bfloat16 [2, 768, 768], P(None, ('head', 'blk')), may hold values from -0.21875 to 0.21875
- w_out: bfloat16 [2, 768, 768], P(None, ('head', 'blk')), may hold values from -1.25 to 1.25
- w_in: bfloat16 [2, 768, 3072], P(None, ('head', 'blk')), may hold values from -0.21875 to 0.21875
- w_down: bfloat16 [2, 3072, 768], P(None, ('head', 'blk')), may hold values from -0.109375 to 0.109375
- b_query: bfloat16 [2, 768], P(None, ('head', 'blk')), may hold values from -3 to 3
- b_value: bfloat16 [2, 768], P(None, ('head', 'blk')), may hold values from -3 to 3
- b_out: bfloat16 [2, 768], P(None, ('head', 'blk')), may hold values from -3 to 3
- b_in: bfloat16 [2, 3072], P(None, ('head', 'blk')), may hold values from -3 to 3
- b_down: bfloat16 [2, 768], P(None, ('head', 'blk')), may hold values from -3 to 3
- norm1_gain: bfloat16 [2, 768], P(None, ('head', 'blk')), may hold values from 0.5 to 1.5
- norm1_bias: bfloat16 [2, 768], P(None, ('head', 'blk')), may hold values from -2 to 2
- norm2_gain: bfloat16 [2, 768], P(None, ('head', 'blk')), may hold values from 0.5 to 1.5
- norm2_bias: bfloat16 [2, 768], P(None, ('head', 'blk')), may hold values from -2 to 2
Outputs:
- block_out: float32 [8, 1024, 768], P('head', 'blk')
- grad_tokens: float32 [8, 1024, 768], P('head', 'blk')
- grad_w_query: float32 [2, 768, 768], P(None, ('head', 'blk'))
- grad_w_key: float32 [2, 768, 768], P(None, ('head', 'blk'))
- grad_w_value: float32 [2, 768, 768], P(None, ('head', 'blk'))
- grad_w_out: float32 [2, 768, 768], P(None, ('head', 'blk'))
- grad_w_in: float32 [2, 768, 3072], P(None, ('head', 'blk'))
- grad_w_down: float32 [2, 3072, 768], P(None, ('head', 'blk'))
- grad_b_query: float32 [2, 768], P(None, ('head', 'blk'))
- grad_b_value: float32 [2, 768], P(None, ('head', 'blk'))
- grad_b_out: float32 [2, 768], P(None, ('head', 'blk'))
- grad_b_in: float32 [2, 3072], P(None, ('head', 'blk'))
- grad_b_down: float32 [2, 768], P(None, ('head', 'blk'))
- grad_norm1_gain: float32 [2, 768], P(None, ('head', 'blk'))
- grad_norm1_bias: float32 [2, 768], P(None, ('head', 'blk'))
- grad_norm2_gain: float32 [2, 768], P(None, ('head', 'blk'))
- grad_norm2_bias: float32 [2, 768], P(None, ('head', 'blk'))
The draws below stay inside these ranges and needn't reach their ends.
Inputs may be any that keep to these rules, and one draw needn't show every extreme that they name: lengths[i] is the number of valid leading positions of sequence i; in every draw one sequence has 1024 of them and one has 256. `slot_sequence`: a permutation of the sequences over the slots.
All inputs are finite; a program needn't handle non-finite values.
Results may differ from the reference program's by a relative error of at most 0.03.
Values may be sent and summed in bfloat16 or wider, within the bound.
A program may use at most 320 MiB of HBM per device.

```python
import jax
import jax.numpy as jnp
from jax import lax

D = 768
FF = 3072
H = 12
DH = 64
LAYERS = 2
SLOTS = 8
L = 1024


def draw_lengths(key, part):
    first_key, second_key = jax.random.split(key)
    values = jax.random.randint(first_key, (SLOTS,), L // 4, L + 1)
    order = jax.random.permutation(second_key, SLOTS)
    values = values.at[order[0]].set(L)
    values = values.at[order[1]].set(L // 4)
    return values.astype(jnp.int32)


def strengthened(array, key, source, target, shards_of, factor):
    owner, partner = [(jnp.arange(array.shape[dim]) // (array.shape[dim] // shards_of)).reshape([-1 if axis == dim else 1 for axis in range(array.ndim)]) for dim in (source, target)]
    chosen = jax.random.permutation(key, shards_of)[partner]
    strong = (owner == chosen) | (owner == (partner + shards_of // 2) % shards_of)
    return jnp.where(strong, factor * array, array)


def shard_levels(rng, shape, shards, least, high):
    def one(position, shards_of):
        steps = jax.random.uniform(jax.random.fold_in(jax.random.fold_in(rng, 6), position), (shards_of,), jnp.float32, least / len(shards), high / len(shards))
        return jnp.repeat(jnp.exp(steps), shape[position] // shards_of).reshape((-1,) + (1,) * (len(shape) - position - 1))

    loudness = one(*shards[0])
    for cut in shards[1:]:
        loudness = loudness * one(*cut)
    return loudness


def centred(rng, dims, deviation, reach, pieces=(), held_as=jnp.bfloat16):
    values = jax.random.normal(rng, dims, jnp.float32) * deviation
    if len(pieces) > 0:
        values = shard_levels(rng, dims, pieces, -0.22, 0.18) * values
    return jnp.clip(values, min=-reach, max=reach).astype(held_as)


def heavy_noise(key, shape, deviation, reach, shards, heavy, dtype=jnp.bfloat16):
    values = deviation * jax.random.normal(key, shape, jnp.float32)
    if shards:
        values = values * shard_levels(key, shape, shards, -0.22, 0.18)
    return jnp.clip(strengthened(values, jax.random.fold_in(key, 3), *heavy), -reach, reach).astype(dtype)


def setup_inputs(seed: int = 0) -> dict:
    keys = jax.random.split(jax.random.key(seed), 20)
    return {
        "tokens": centred(keys[0], (SLOTS, L, D), 1.0, 6.0, ((0, 4), (1, 8))),
        "lengths": draw_lengths(jax.random.fold_in(keys[19], 71), 0),
        "slot_sequence": jax.random.permutation(keys[2], SLOTS).astype(jnp.int32),
        "cotangent": heavy_noise(keys[3], (SLOTS, L, D), 1.0, 6.0, ((0, 4), (1, 8)), (1, 2, 8, 2.0)),
        "w_query": centred(keys[4], (LAYERS, D, D), (D // 2) ** -0.5, 0.3125, ((1, 32),)),
        "w_key": centred(keys[5], (LAYERS, D, D), (D // 2) ** -0.5, 0.3125, ((1, 32),)),
        "w_value": centred(keys[6], (LAYERS, D, D), D ** -0.5, 0.21875, ((1, 32),)),
        "w_out": centred(keys[7], (LAYERS, D, D), (D // 32) ** -0.5, 1.25, ((1, 32),)),
        "w_in": centred(keys[8], (LAYERS, D, FF), D ** -0.5, 0.21875, ((1, 32),)),
        "w_down": centred(keys[9], (LAYERS, FF, D), FF ** -0.5, 0.109375, ((1, 32),)),
        "b_query": centred(keys[10], (LAYERS, D), 0.5, 3.0, ((1, 32),)),
        "b_value": centred(keys[11], (LAYERS, D), 0.5, 3.0, ((1, 32),)),
        "b_out": centred(keys[12], (LAYERS, D), 0.5, 3.0, ((1, 32),)),
        "b_in": centred(keys[13], (LAYERS, FF), 0.5, 3.0, ((1, 32),)),
        "b_down": centred(keys[14], (LAYERS, D), 0.5, 3.0, ((1, 32),)),
        "norm1_gain": jnp.clip(1.0 + 0.1 * jax.random.normal(keys[15], (LAYERS, D), jnp.float32), 0.5, 1.5).astype(jnp.bfloat16),
        "norm1_bias": centred(keys[16], (LAYERS, D), 0.3, 2.0, ((1, 32),)),
        "norm2_gain": jnp.clip(1.0 + 0.1 * jax.random.normal(keys[17], (LAYERS, D), jnp.float32), 0.5, 1.5).astype(jnp.bfloat16),
        "norm2_bias": centred(keys[18], (LAYERS, D), 0.3, 2.0, ((1, 32),)),
    }


EPS = 1e-05
NEG = -1e+30

@jax.custom_vjp
def low(v):
    return lax.optimization_barrier(v.astype(jnp.bfloat16)).astype(jnp.float32)

@jax.custom_vjp
def low_back(v):
    return v

def low_keep(v):
    return (low(v), None)

def low_pass(kept, grad):
    return (grad,)

def back_keep(v):
    return (v, None)

def back_low(kept, grad):
    return (low(grad),)
low.defvjp(low_keep, low_pass)
low_back.defvjp(back_keep, back_low)

def matmul(former, latter):
    return jnp.dot(former, latter, precision=lax.Precision.HIGHEST)

def layer_norm(stream, factor, offset):
    centre = stream - lax.optimization_barrier(jnp.mean(stream, axis=-1, keepdims=True))
    spread = lax.rsqrt(lax.optimization_barrier(jnp.mean(centre * centre, axis=-1, keepdims=True)) + EPS)
    return centre * spread * factor + offset

def attend(queries, key_rows, value_rows, key_valid):
    scores = low_back(matmul(queries, key_rows.T) * 0.125)
    scores = jnp.where(key_valid[None, :], scores, NEG)
    log_norm = jax.nn.logsumexp(scores, axis=1, keepdims=True)
    probs = jnp.exp(scores - log_norm)
    return matmul(low(probs), value_rows)

def one_layer(hidden, weights, key_valid):
    mat_query, mat_key, mat_value, mat_out, mat_in, mat_down, bias_query, bias_value, bias_out, bias_in, bias_down, gain_one, shift_one, gain_two, shift_two = weights
    length = hidden.shape[0]
    inputs = low(hidden)
    queries = low_back(low(matmul(inputs, mat_query) + bias_query))
    key_rows = low_back(low(matmul(inputs, mat_key)))
    value_rows = low_back(low(matmul(inputs, mat_value) + bias_value))

    def split(matrix):
        return jnp.transpose(matrix.reshape(length, H, DH), (1, 0, 2))

    def head_fn(bundle):
        return attend(bundle[0], bundle[1], bundle[2], key_valid)
    heads = lax.map(jax.checkpoint(head_fn), (split(queries), split(key_rows), split(value_rows)))
    context = low_back(low(jnp.transpose(heads, (1, 0, 2)).reshape(length, H * DH)))
    first = hidden + low_back(matmul(context, mat_out) + bias_out)
    normed_one = layer_norm(first, gain_one, shift_one)
    pre_act = low_back(matmul(low(normed_one), mat_in) + bias_in)
    activated = low(jax.nn.gelu(pre_act, approximate=False))
    second = normed_one + low_back(matmul(activated, mat_down) + bias_down)
    return layer_norm(second, gain_two, shift_two)

def reference(tokens, lengths, slot_sequence, cotangent, w_query, w_key, w_value, w_out, w_in, w_down, b_query, b_value, b_out, b_in, b_down, norm1_gain, norm1_bias, norm2_gain, norm2_bias):
    slot_ids = lax.iota(jnp.int32, SLOTS)
    slot_len = lax.optimization_barrier(jnp.sum(jnp.where(slot_sequence[:, None] == slot_ids[None, :], lengths[None, :], 0), axis=1))
    params = tuple((item.astype(jnp.float32) for item in (w_query, w_key, w_value, w_out, w_in, w_down, b_query, b_value, b_out, b_in, b_down, norm1_gain, norm1_bias, norm2_gain, norm2_bias)))
    positions = lax.iota(jnp.int32, L)

    def model(weights, hidden, key_valid):
        for layer_index in range(LAYERS):
            hidden = one_layer(hidden, tuple((item[layer_index] for item in weights)), key_valid)
        return hidden

    def per_slot(totals, inputs):
        slot_tokens, slot_back, length = inputs
        key_valid = positions < length

        def forward(weights, hidden):
            return model(weights, hidden, key_valid)
        result, pull = jax.vjp(forward, params, slot_tokens.astype(jnp.float32))
        row_scale = jnp.where(key_valid, 1.0, 0.0).astype(jnp.float32)
        grads, back_tokens = pull(slot_back.astype(jnp.float32) * row_scale[:, None])
        totals = jax.tree.map(lambda former, latter: former + latter, totals, grads)
        return (totals, (result, back_tokens))
    zeros = jax.tree.map(jnp.zeros_like, params)
    totals, (block_out, grad_tokens) = lax.scan(per_slot, zeros, (tokens, cotangent, slot_len))
    return (block_out, grad_tokens, totals[0], totals[1], totals[2], totals[3], totals[4], totals[5], totals[6], totals[7], totals[8], totals[9], totals[10], totals[11], totals[12], totals[13], totals[14])
```

```python
from functools import partial
import math

import jax
import jax.numpy as jnp
from jax import lax
from jax.experimental import pallas as pl
from jax.experimental.pallas import tpu as pltpu
from jax.sharding import Mesh, PartitionSpec as P

H = 12
DH = 64
LAYERS = 2


EPS = 1e-05
NEG = -1e30


def dot_plain(former, latter):
    return jnp.dot(former, latter, preferred_element_type=jnp.float32)


def dot_right_t(former, latter):
    return lax.dot_general(
        former, latter, (((1,), (1,)), ((), ())), preferred_element_type=jnp.float32
    )


def dot_left_t(former, latter):
    return lax.dot_general(
        former, latter, (((0,), (0,)), ((), ())), preferred_element_type=jnp.float32
    )


def layer_norm(stream, factor, offset):
    centre = stream - jnp.mean(stream, axis=-1, keepdims=True)
    spread = lax.rsqrt(jnp.mean(centre * centre, axis=-1, keepdims=True) + EPS)
    normed = centre * spread
    return (normed * factor + offset, normed, spread)


def norm_back(upstream, normed, spread, factor):
    scaled = upstream * factor
    inner = (
        scaled
        - jnp.mean(scaled, axis=-1, keepdims=True)
        - normed * jnp.mean(scaled * normed, axis=-1, keepdims=True)
    )
    return (inner * spread, jnp.sum(upstream * normed, 0), jnp.sum(upstream, 0))


def pair_scores(queries, key_rows):
    return (
        jnp.einsum("sqhd,skhd->sqhk", queries, key_rows, preferred_element_type=jnp.float32) * 0.125
    )


def key_valid(start, count, slot_len):
    positions = start + lax.iota(jnp.int32, count)
    return (positions[None, :] < slot_len[:, None])[:, None, None, :]


def over_blocks(state, pieces, step_fn):
    width = pieces[0].shape[1]
    size = math.gcd(width, 512)

    def one_block(index, carry):
        offset = index * size
        parts = tuple((lax.dynamic_slice_in_dim(item, offset, size, 1) for item in pieces))
        return step_fn(carry, parts, offset)

    return lax.fori_loop(0, width // size, one_block, state)


def attention_forward(head_query, head_keys, head_values, slot_len):
    slots, rows, heads, _ = head_query.shape

    def max_step(carry, parts, start):
        peak, total = carry
        scores = jnp.where(
            key_valid(start, parts[0].shape[1], slot_len), pair_scores(head_query, parts[0]), NEG
        )
        top = jnp.maximum(peak, jnp.max(scores, -1))
        total = total * jnp.exp(peak - top) + jnp.sum(jnp.exp(scores - top[..., None]), -1)
        return (top, total)

    start_state = (
        jnp.full((slots, rows, heads), NEG, jnp.float32),
        jnp.zeros((slots, rows, heads), jnp.float32),
    )
    peak, total = over_blocks(
        start_state, (lax.all_gather(head_keys, "blk", axis=1, tiled=True),), max_step
    )
    log_norm = peak + jnp.log(total)

    def value_step(carry, parts, start):
        summed, fixed = carry
        key_part, value_part = parts
        scores = jnp.where(
            key_valid(start, key_part.shape[1], slot_len), pair_scores(head_query, key_part), NEG
        )
        probs = jnp.exp(scores - log_norm[..., None])
        rounded = probs.astype(jnp.bfloat16)
        remainder = (probs - rounded.astype(jnp.float32)).astype(jnp.bfloat16)
        summed = summed + jnp.einsum(
            "sqhk,skhd->sqhd", rounded, value_part, preferred_element_type=jnp.float32
        )
        fixed = fixed + jnp.einsum(
            "sqhk,skhd->sqhd", remainder, value_part, preferred_element_type=jnp.float32
        )
        return (summed, fixed)

    zeros = jnp.zeros(head_query.shape, jnp.float32)
    summed, fixed = over_blocks(
        (zeros, zeros),
        (
            lax.all_gather(head_keys, "blk", axis=1, tiled=True),
            lax.all_gather(head_values, "blk", axis=1, tiled=True),
        ),
        value_step,
    )
    return (log_norm, summed, summed + fixed)


def attention_backward(
    head_query, head_keys, head_values, back_heads, log_norm, delta, slot_len, own_valid
):

    def query_step(carry, parts, start):
        key_part, value_part = parts
        scores = jnp.where(
            key_valid(start, key_part.shape[1], slot_len), pair_scores(head_query, key_part), NEG
        )
        probs = jnp.exp(scores - log_norm[..., None])
        slope = jnp.einsum(
            "sqhd,skhd->sqhk", back_heads, value_part, preferred_element_type=jnp.float32
        )
        score_back = (probs * (slope - delta[..., None])).astype(jnp.bfloat16)
        return carry + jnp.einsum(
            "sqhk,skhd->sqhd", score_back, key_part, preferred_element_type=jnp.float32
        )

    zeros = jnp.zeros(head_query.shape, jnp.float32)
    query_sum = over_blocks(
        zeros,
        (
            lax.all_gather(head_keys, "blk", axis=1, tiled=True),
            lax.all_gather(head_values, "blk", axis=1, tiled=True),
        ),
        query_step,
    )
    all_log, all_delta = (
        lax.all_gather(log_norm, "blk", axis=1, tiled=True),
        lax.all_gather(delta, "blk", axis=1, tiled=True),
    )

    def key_step(carry, parts, start):
        key_sum, value_sum = carry
        query_part, back_part = parts
        count = query_part.shape[1]
        log_part = lax.dynamic_slice_in_dim(all_log, start, count, 1)
        delta_part = lax.dynamic_slice_in_dim(all_delta, start, count, 1)
        scores = jnp.where(own_valid, pair_scores(query_part, head_keys), NEG)
        probs = jnp.exp(scores - log_part[..., None])
        rounded = probs.astype(jnp.bfloat16)
        value_sum = value_sum + jnp.einsum(
            "sqhk,sqhd->skhd", rounded, back_part, preferred_element_type=jnp.float32
        )
        slope = jnp.einsum(
            "sqhd,skhd->sqhk", back_part, head_values, preferred_element_type=jnp.float32
        )
        score_back = (probs * (slope - delta_part[..., None])).astype(jnp.bfloat16)
        key_sum = key_sum + jnp.einsum(
            "sqhk,sqhd->skhd", score_back, query_part, preferred_element_type=jnp.float32
        )
        return (key_sum, value_sum)

    key_sum, value_sum = over_blocks(
        (zeros, zeros),
        (
            lax.all_gather(head_query, "blk", axis=1, tiled=True),
            lax.all_gather(back_heads, "blk", axis=1, tiled=True),
        ),
        key_step,
    )
    return (
        (query_sum * 0.125).astype(jnp.bfloat16),
        (key_sum * 0.125).astype(jnp.bfloat16),
        value_sum.astype(jnp.bfloat16),
    )


def fetch_forward(shards, layer_index):
    return (
        lax.all_gather(shards[0][layer_index], ("head", "blk"), axis=0, tiled=True),
        lax.all_gather(shards[1][layer_index], ("head", "blk"), axis=0, tiled=True),
        lax.all_gather(shards[2][layer_index], ("head", "blk"), axis=0, tiled=True),
        lax.all_gather(shards[3][layer_index], ("head", "blk"), axis=0, tiled=True),
        lax.all_gather(shards[4][layer_index], ("head", "blk"), axis=0, tiled=True),
        lax.all_gather(shards[5][layer_index], ("head", "blk"), axis=0, tiled=True),
        lax.all_gather(shards[6][layer_index], ("head", "blk"), axis=0, tiled=True),
        lax.all_gather(shards[7][layer_index], ("head", "blk"), axis=0, tiled=True),
        lax.all_gather(shards[8][layer_index], ("head", "blk"), axis=0, tiled=True),
        lax.all_gather(shards[9][layer_index], ("head", "blk"), axis=0, tiled=True),
        lax.all_gather(shards[10][layer_index], ("head", "blk"), axis=0, tiled=True),
        lax.all_gather(shards[11][layer_index], ("head", "blk"), axis=0, tiled=True),
        lax.all_gather(shards[12][layer_index], ("head", "blk"), axis=0, tiled=True),
        lax.all_gather(shards[13][layer_index], ("head", "blk"), axis=0, tiled=True),
        lax.all_gather(shards[14][layer_index], ("head", "blk"), axis=0, tiled=True),
    )


def fetch_backward(shards, layer_index):
    return (
        lax.all_gather(shards[0][layer_index], ("head", "blk"), axis=0, tiled=True),
        lax.all_gather(shards[1][layer_index], ("head", "blk"), axis=0, tiled=True),
        lax.all_gather(shards[2][layer_index], ("head", "blk"), axis=0, tiled=True),
        lax.all_gather(shards[3][layer_index], ("head", "blk"), axis=0, tiled=True),
        lax.all_gather(shards[4][layer_index], ("head", "blk"), axis=0, tiled=True),
        lax.all_gather(shards[5][layer_index], ("head", "blk"), axis=0, tiled=True),
        lax.all_gather(shards[6][layer_index], ("head", "blk"), axis=0, tiled=True),
        lax.all_gather(shards[7][layer_index], ("head", "blk"), axis=0, tiled=True),
        lax.all_gather(shards[8][layer_index], ("head", "blk"), axis=0, tiled=True),
        lax.all_gather(shards[9][layer_index], ("head", "blk"), axis=0, tiled=True),
        lax.all_gather(shards[10][layer_index], ("head", "blk"), axis=0, tiled=True),
        lax.all_gather(shards[11][layer_index], ("head", "blk"), axis=0, tiled=True),
        lax.all_gather(shards[12][layer_index], ("head", "blk"), axis=0, tiled=True),
        lax.all_gather(shards[13][layer_index], ("head", "blk"), axis=0, tiled=True),
        lax.all_gather(shards[14][layer_index], ("head", "blk"), axis=0, tiled=True),
    )


def pack_rows(terms, owners):
    rows = []
    shapes = []
    for term in terms:
        shapes.append((term.shape[0] // owners,) + term.shape[1:])
        flat = term.reshape(owners, -1)
        rows.append(flat)
    return (jnp.concatenate(rows, 1), shapes)


def unpack_row(summed, shapes):
    pieces = []
    offset = 0
    for shape in shapes:
        count = math.prod(shape)
        pieces.append(summed[0, offset : offset + count].reshape(shape))
        offset = offset + count
    return tuple(pieces)


def scatter_layer(terms, owners):
    packed, shapes = pack_rows(terms, owners)
    summed = lax.psum_scatter(packed, ("head", "blk"), scatter_dimension=0, tiled=True)
    return unpack_row(summed, shapes)


def per_device(
    tokens,
    lengths,
    slot_sequence,
    cotangent,
    w_query,
    w_key,
    w_value,
    w_out,
    w_in,
    w_down,
    b_query,
    b_value,
    b_out,
    b_in,
    b_down,
    norm1_gain,
    norm1_bias,
    norm2_gain,
    norm2_bias,
):
    slots_here, local, width = tokens.shape
    head_count = lax.axis_size("head")
    owners = head_count * lax.axis_size("blk")
    heads = H // head_count
    all_slots = lengths.shape[0]
    slot_ids = lax.iota(jnp.int32, all_slots)
    slot_len = jnp.sum(
        jnp.where(slot_sequence[:, None] == slot_ids[None, :], lengths[None, :], 0), axis=1
    )
    own_ids = lax.axis_index("head") * slots_here + lax.iota(jnp.int32, slots_here)
    own_len = jnp.sum(
        jnp.where(own_ids[:, None] == slot_ids[None, :], slot_len[None, :], 0), axis=1
    )
    token_pos = lax.axis_index("blk") * local + lax.iota(jnp.int32, local)
    row_valid = jnp.where(token_pos[None, :] < own_len[:, None], 1.0, 0.0).astype(jnp.float32)
    own_valid = key_valid(lax.axis_index("blk") * local, local, slot_len)
    shards = (
        w_query,
        w_key,
        w_value,
        w_out,
        w_in,
        w_down,
        b_query,
        b_value,
        b_out,
        b_in,
        b_down,
        norm1_gain,
        norm1_bias,
        norm2_gain,
        norm2_bias,
    )
    hidden = tokens.astype(jnp.float32)
    kept_list = []
    weight_list = []
    for layer_index in range(LAYERS):
        weights = fetch_forward(shards, layer_index)
        (
            forward_mat_query,
            forward_mat_key,
            forward_mat_value,
            forward_mat_out,
            forward_mat_in,
            forward_mat_down,
            forward_bias_query,
            forward_bias_value,
            forward_bias_out,
            forward_bias_in,
            forward_bias_down,
            forward_gain_one,
            forward_shift_one,
            forward_gain_two,
            forward_shift_two,
        ) = weights
        flat = hidden.reshape(slots_here * local, width)
        forward_inputs = flat.astype(jnp.bfloat16)
        queries = (dot_plain(forward_inputs, forward_mat_query) + forward_bias_query).astype(
            jnp.bfloat16
        )
        key_rows = dot_plain(forward_inputs, forward_mat_key).astype(jnp.bfloat16)
        value_rows = (dot_plain(forward_inputs, forward_mat_value) + forward_bias_value).astype(
            jnp.bfloat16
        )
        forward_stacked = jnp.stack([queries, key_rows, value_rows], 1).reshape(
            slots_here, local, 3, width
        )
        grouped = lax.all_to_all(forward_stacked, "head", split_axis=3, concat_axis=0, tiled=True)
        headed = grouped.reshape(all_slots, local, 3, heads, DH)
        forward_head_query = headed[:, :, 0]
        forward_head_keys = headed[:, :, 1]
        forward_head_values = headed[:, :, 2]
        forward_log_norm, summed, forward_exact = attention_forward(
            forward_head_query, forward_head_keys, forward_head_values, slot_len
        )
        context_head = summed.astype(jnp.bfloat16).reshape(all_slots, local, heads * DH)
        forward_context = lax.all_to_all(
            context_head, "head", split_axis=0, concat_axis=2, tiled=True
        ).reshape(slots_here * local, width)
        first = flat + dot_plain(forward_context, forward_mat_out) + forward_bias_out
        normed_one, forward_hat_one, forward_spread_one = layer_norm(
            first, forward_gain_one.astype(jnp.float32), forward_shift_one.astype(jnp.float32)
        )
        forward_ff_in = normed_one.astype(jnp.bfloat16)
        forward_pre_act = dot_plain(forward_ff_in, forward_mat_in) + forward_bias_in
        forward_activated = jax.nn.gelu(forward_pre_act, approximate=False).astype(jnp.bfloat16)
        second = normed_one + dot_plain(forward_activated, forward_mat_down) + forward_bias_down
        result, forward_hat_two, forward_spread_two = layer_norm(
            second, forward_gain_two.astype(jnp.float32), forward_shift_two.astype(jnp.float32)
        )
        forward_kept = (
            forward_inputs,
            forward_head_query,
            forward_head_keys,
            forward_head_values,
            forward_log_norm,
            forward_exact,
            forward_context,
            forward_hat_one,
            forward_spread_one,
            forward_ff_in,
            forward_pre_act,
            forward_activated,
            forward_hat_two,
            forward_spread_two,
        )
        hidden = result.reshape(slots_here, local, width)
        kept_list.append(forward_kept)
        weight_list.append(weights)
    back = (cotangent.astype(jnp.float32) * row_valid[:, :, None]).reshape(
        slots_here * local, width
    )
    grad_layers = [None] * LAYERS
    for layer_index in reversed(range(LAYERS)):
        weights = fetch_backward(shards, layer_index)
        (
            mat_query,
            mat_key,
            mat_value,
            mat_out,
            mat_in,
            mat_down,
            bias_query,
            bias_value,
            bias_out,
            bias_in,
            bias_down,
            gain_one,
            shift_one,
            gain_two,
            shift_two,
        ) = weights
        (
            inputs,
            head_query,
            head_keys,
            head_values,
            log_norm,
            exact,
            context,
            hat_one,
            spread_one,
            ff_in,
            pre_act,
            activated,
            hat_two,
            spread_two,
        ) = kept_list[layer_index]
        back_second, grad_gain_two, grad_shift_two = norm_back(
            back, hat_two, spread_two, gain_two.astype(jnp.float32)
        )
        back_down = back_second.astype(jnp.bfloat16)
        grad_mat_down = dot_left_t(activated, back_down)
        grad_bias_down = jnp.sum(back_down.astype(jnp.float32), 0)
        back_act = dot_right_t(back_down, mat_down)
        gelu_pull = jax.vjp(partial(jax.nn.gelu, approximate=False), pre_act)[1]
        back_pre = gelu_pull(back_act)[0].astype(jnp.bfloat16)
        grad_mat_in = dot_left_t(ff_in, back_pre)
        grad_bias_in = jnp.sum(back_pre.astype(jnp.float32), 0)
        back_normed = back_second + dot_right_t(back_pre, mat_in)
        back_first, grad_gain_one, grad_shift_one = norm_back(
            back_normed, hat_one, spread_one, gain_one.astype(jnp.float32)
        )
        back_branch = back_first.astype(jnp.bfloat16)
        grad_mat_out = dot_left_t(context, back_branch)
        grad_bias_out = jnp.sum(back_branch.astype(jnp.float32), 0)
        back_context = (
            dot_right_t(back_branch, mat_out).astype(jnp.bfloat16).reshape(slots_here, local, width)
        )
        back_heads = lax.all_to_all(
            back_context, "head", split_axis=2, concat_axis=0, tiled=True
        ).reshape(all_slots, local, heads, DH)
        delta = jnp.sum(back_heads.astype(jnp.float32) * exact, -1)
        query_back, key_back, value_back = attention_backward(
            head_query, head_keys, head_values, back_heads, log_norm, delta, slot_len, own_valid
        )
        stacked = jnp.stack([query_back, key_back, value_back], 2).reshape(
            all_slots, local, 3, heads * DH
        )
        joined = lax.all_to_all(stacked, "head", split_axis=0, concat_axis=3, tiled=True).reshape(
            slots_here * local, 3, width
        )
        back_query = joined[:, 0]
        back_key = joined[:, 1]
        back_value = joined[:, 2]
        grad_mat_query = dot_left_t(inputs, back_query)
        grad_mat_key = dot_left_t(inputs, back_key)
        grad_mat_value = dot_left_t(inputs, back_value)
        grad_bias_query = jnp.sum(back_query.astype(jnp.float32), 0)
        grad_bias_value = jnp.sum(back_value.astype(jnp.float32), 0)
        back_hidden = (
            back_first
            + dot_right_t(back_query, mat_query)
            + dot_right_t(back_key, mat_key)
            + dot_right_t(back_value, mat_value)
        )
        terms = (
            grad_mat_query,
            grad_mat_key,
            grad_mat_value,
            grad_mat_out,
            grad_mat_in,
            grad_mat_down,
            grad_bias_query,
            grad_bias_value,
            grad_bias_out,
            grad_bias_in,
            grad_bias_down,
            grad_gain_one,
            grad_shift_one,
            grad_gain_two,
            grad_shift_two,
        )
        back, terms = (back_hidden, terms)
        grad_layers[layer_index] = scatter_layer(terms, owners)
    grads = tuple(
        (jnp.stack([grad_layers[index][member] for index in range(LAYERS)]) for member in range(15))
    )
    return (hidden, back.reshape(slots_here, local, width)) + tuple(grads)


def plain_solution(mesh):
    placed = (
        P("head", "blk", None),
        P(),
        P(),
        P("head", "blk", None),
        P(None, ("head", "blk"), None),
        P(None, ("head", "blk"), None),
        P(None, ("head", "blk"), None),
        P(None, ("head", "blk"), None),
        P(None, ("head", "blk"), None),
        P(None, ("head", "blk"), None),
        P(None, ("head", "blk")),
        P(None, ("head", "blk")),
        P(None, ("head", "blk")),
        P(None, ("head", "blk")),
        P(None, ("head", "blk")),
        P(None, ("head", "blk")),
        P(None, ("head", "blk")),
        P(None, ("head", "blk")),
        P(None, ("head", "blk")),
    )
    return jax.shard_map(
        per_device,
        mesh=mesh,
        in_specs=placed,
        out_specs=(
            P("head", "blk", None),
            P("head", "blk", None),
            P(None, ("head", "blk"), None),
            P(None, ("head", "blk"), None),
            P(None, ("head", "blk"), None),
            P(None, ("head", "blk"), None),
            P(None, ("head", "blk"), None),
            P(None, ("head", "blk"), None),
            P(None, ("head", "blk")),
            P(None, ("head", "blk")),
            P(None, ("head", "blk")),
            P(None, ("head", "blk")),
            P(None, ("head", "blk")),
            P(None, ("head", "blk")),
            P(None, ("head", "blk")),
            P(None, ("head", "blk")),
            P(None, ("head", "blk")),
        ),
        check_vma=False,
    )


MESH_ID = pl.DeviceIdType.MESH
AXES = ("x", "c", "z", "y")
NX, NC, NZ, NY = 2, 2, 4, 2
F32 = jnp.float32
BF16 = jnp.bfloat16


def place():
    return tuple(lax.axis_index(name) for name in AXES)


class Sems:
    def __init__(self, ref):
        self.ref = ref
        self.used = 0

    def take(self):
        self.used += 1
        return self.ref.at[self.used - 1]


def enter_barrier():
    x, c, z, y = place()
    barrier = pltpu.get_barrier_semaphore()
    peers = [(1 - x, c, z, y), (x, c, z, 1 - y)]
    for dz in range(NZ):
        for dc in range(NC):
            if dz or dc:
                peers.append((x, (c + dc) % NC, (z + dz) % NZ, y))
    for peer in peers:
        pl.semaphore_signal(barrier, inc=1, device_id=peer, device_id_type=MESH_ID)
    pl.semaphore_wait(barrier, len(peers))


def remote(src, dst, sems, peer):
    return pltpu.make_async_remote_copy(
        src_ref=src,
        dst_ref=dst,
        send_sem=sems.take(),
        recv_sem=sems.take(),
        device_id=peer,
        device_id_type=MESH_ID,
    )


class Gather:
    def __init__(self, kind, src, dst, sems):
        self.kind, self.src, self.dst = kind, src, dst
        x, c, z, y = place()
        self.first = []
        if kind == "row":
            here = dst.at[x, z, y]
            self.local = pltpu.make_async_copy(src, here, sems.take())
            for dz in range(1, NZ):
                self.first.append(remote(src, here, sems, (x, c, (z + dz) % NZ, y)))
            mine = dst.at[x, :, y]
            via_y = dst.at[1 - x, 0:2, y]
            via_x = dst.at[x, 2:4, 1 - y]
        else:
            here = dst.at[x, c, z, y]
            pick = (lambda core: src.at[core]) if kind == "col" else (lambda core: src)
            self.local = pltpu.make_async_copy(pick(c), here, sems.take())
            for dz in range(NZ):
                for dc in range(NC):
                    if dz or dc:
                        core = (c + dc) % NC
                        self.first.append(remote(pick(core), here, sems, (x, core, (z + dz) % NZ, y)))
            mine = dst.at[x, :, :, y]
            via_y = dst.at[1 - x, 0, :, y]
            via_x = dst.at[x, 1, :, 1 - y]
        self.second = [
            remote(mine, mine, sems, (1 - x, c, z, y)),
            remote(mine, mine, sems, (x, c, z, 1 - y)),
        ]
        self.third = [
            remote(via_y, via_y, sems, (x, c, z, 1 - y)),
            remote(via_x, via_x, sems, (1 - x, c, z, y)),
        ]

    def start_first(self):
        self.local.start()
        for item in self.first:
            item.start()

    def start_second(self):
        self.local.wait()
        for item in self.first:
            item.wait_recv()
        for item in self.second:
            item.start()

    def start_third(self):
        for item in self.second:
            item.wait_recv()
        for item in self.third:
            item.start()

    def finish(self):
        for item in self.third:
            item.wait_recv()
        for item in self.first + self.second + self.third:
            item.wait_send()


class Rows:
    def __init__(self, src, own, other, sems):
        x, c, z, y = place()
        self.other = other
        self.relay = c == z // 2
        self.go, self.stay = [], []
        send = [sems.take(), sems.take()]
        recv = [sems.take() for _ in range(NZ)]
        local = sems.take()
        base = sems.used - NZ - 1
        for i in range(2):
            self.go.append(
                pltpu.make_async_remote_copy(
                    src_ref=src.at[i],
                    dst_ref=own.at[z],
                    send_sem=send[i],
                    recv_sem=sems.ref.at[base + z],
                    device_id=(x, c, 2 * c + i, y),
                    device_id_type=MESH_ID,
                )
            )
            self.stay.append(pltpu.make_async_copy(src.at[i], own.at[z], local))
        self.arrive = []
        for dz in range(1, NZ):
            zs = (z + dz) % NZ
            self.arrive.append(
                pltpu.make_async_remote_copy(
                    src_ref=src.at[0],
                    dst_ref=own.at[zs],
                    send_sem=send[0],
                    recv_sem=sems.ref.at[base + zs],
                    device_id=(x, c, zs, y),
                    device_id_type=MESH_ID,
                )
            )
        self.pass_own = remote(own, own, sems, (x, 1 - c, z, y))
        if other is not None:
            self.cross = remote(own, other, sems, (x, c, z, 1 - y))
            self.pass_other = remote(other, other, sems, (x, 1 - c, z, y))

    def start(self):
        x, c, z, y = place()
        for i in range(2):
            @pl.when(2 * c + i != z)
            def _():
                self.go[i].start()

            @pl.when(2 * c + i == z)
            def _():
                self.stay[i].start()

    def forward(self):
        @pl.when(self.relay)
        def _():
            self.stay[0].wait()
            for item in self.arrive:
                item.wait_recv()
            if self.other is not None:
                self.cross.start()
            self.pass_own.start()

    def forward_other(self):
        if self.other is not None:
            @pl.when(self.relay)
            def _():
                self.cross.wait_recv()
                self.pass_other.start()

    def finish(self):
        x, c, z, y = place()
        for i in range(2):
            @pl.when(2 * c + i != z)
            def _():
                self.go[i].wait_send()

        @pl.when(self.relay)
        def _():
            self.pass_own.wait_send()
            if self.other is not None:
                self.cross.wait_send()
                self.pass_other.wait_send()

        @pl.when(jnp.logical_not(self.relay))
        def _():
            self.pass_own.wait_recv()
            if self.other is not None:
                self.pass_other.wait_recv()


def gather_kernel(qkv, w_in, w_out, w_down, small, tokens, cotangent,
                  qkv0, qkv1, in0, in1, out0, out1, down0, down1, smalls, own, other, back,
                  sem_ref):
    sems = Sems(sem_ref)
    rows = Rows(tokens, own, other, sems)
    back_rows = Rows(cotangent, back, None, sems)
    items = [
        Gather("col", qkv.at[0], qkv0, sems),
        Gather("both", small, smalls, sems),
        Gather("row", w_out.at[0], out0, sems),
        Gather("col", w_in.at[0], in0, sems),
        Gather("row", w_down.at[0], down0, sems),
        Gather("col", qkv.at[1], qkv1, sems),
        Gather("row", w_out.at[1], out1, sems),
        Gather("col", w_in.at[1], in1, sems),
        Gather("row", w_down.at[1], down1, sems),
    ]
    enter_barrier()
    rows.start()
    for item in items:
        item.start_first()
    back_rows.start()
    count = len(items)
    for step in range(count + 1):
        if step < count:
            items[step].start_second()
        if step == 0:
            rows.forward()
        if step >= 1:
            items[step - 1].start_third()
        if step == 2:
            rows.forward_other()
    back_rows.forward()
    for item in items:
        item.finish()
    rows.finish()
    back_rows.finish()


GATHER_SEMS = 260


def gather_all(qkv, w_in, w_out, w_down, small, tokens, cotangent):
    hbm = pl.BlockSpec(memory_space=pl.ANY)
    shapes = [
        (2, 2, 4, 2, 24, 1152), (2, 2, 4, 2, 24, 1152),
        (2, 2, 4, 2, 24, 1536), (2, 2, 4, 2, 24, 1536),
        (2, 4, 2, 24, 768), (2, 4, 2, 24, 768),
        (2, 4, 2, 96, 768), (2, 4, 2, 96, 768),
        (2, 2, 4, 2, 8, 128),
        (4, 128, 768), (4, 128, 768), (4, 128, 768),
    ]
    return pl.pallas_call(
        gather_kernel,
        out_shape=[jax.ShapeDtypeStruct(s, BF16) for s in shapes],
        in_specs=[hbm] * 7,
        out_specs=[hbm] * len(shapes),
        scratch_shapes=[pltpu.SemaphoreType.DMA((GATHER_SEMS,))],
        compiler_params=pltpu.CompilerParams(collective_id=0, has_side_effects=True),
        name="gather_all",
    )(qkv, w_in, w_out, w_down, small, tokens, cotangent)


class Reduce:
    def __init__(self, kind, part, sems, first, second, third, out):
        x, c, z, y = place()
        self.kind, self.part, self.out = kind, part, out
        self.first_buf, self.second_buf, self.third_buf = first, second, third
        if kind == "row":
            via_y, via_x = part.at[1 - x, 0:2, 1 - y], part.at[1 - x, 2:4, 1 - y]
            to_x, to_y = part.at[1 - x, :, y], part.at[x, :, 1 - y]
        else:
            via_y, via_x = part.at[1 - x, 0, :, 1 - y], part.at[1 - x, 1, :, 1 - y]
            to_x, to_y = part.at[1 - x, :, :, y], part.at[x, :, :, 1 - y]
        self.first = [
            remote(via_y, first.at[0], sems, (x, c, z, 1 - y)),
            remote(via_x, first.at[1], sems, (1 - x, c, z, y)),
        ]
        self.second = [
            remote(to_x, second.at[0], sems, (1 - x, c, z, y)),
            remote(to_y, second.at[1], sems, (x, c, z, 1 - y)),
        ]
        self.third = []
        if kind == "row":
            for dz in range(1, NZ):
                zt = (z + dz) % NZ
                self.third.append(remote(part.at[x, zt, y], third.at[z], sems, (x, c, zt, y)))
            self.local = pltpu.make_async_copy(part.at[x, z, y], third.at[z], sems.take())
        else:
            for dz in range(NZ):
                for dc in range(NC):
                    if dz or dc:
                        zt, core = (z + dz) % NZ, (c + dc) % NC
                        self.third.append(
                            remote(part.at[x, core, zt, y], third.at[z, c], sems, (x, core, zt, y))
                        )
            self.local = pltpu.make_async_copy(part.at[x, c, z, y], third.at[z, c], sems.take())

    def start_first(self):
        for item in self.first:
            item.start()

    def start_second(self):
        x, c, z, y = place()
        part, first = self.part, self.first_buf
        for item in self.first:
            item.wait_recv()
        if self.kind == "row":
            def add(k, carry):
                part[1 - x, k, y] = (part[1 - x, k, y].astype(F32) + first[0, k].astype(F32)).astype(BF16)
                part[x, 2 + k, 1 - y] = (part[x, 2 + k, 1 - y].astype(F32) + first[1, k].astype(F32)).astype(BF16)
                return carry
            lax.fori_loop(0, 2, add, 0)
        else:
            def add(k, carry):
                part[1 - x, 0, k, y] = (part[1 - x, 0, k, y].astype(F32) + first[0, k].astype(F32)).astype(BF16)
                part[x, 1, k, 1 - y] = (part[x, 1, k, 1 - y].astype(F32) + first[1, k].astype(F32)).astype(BF16)
                return carry
            lax.fori_loop(0, 4, add, 0)
        for item in self.second:
            item.start()

    def start_third(self):
        x, c, z, y = place()
        part, second = self.part, self.second_buf
        for item in self.second:
            item.wait_recv()
        if self.kind == "row":
            def add(k, carry):
                part[x, k, y] = (
                    part[x, k, y].astype(F32) + second[0, k].astype(F32) + second[1, k].astype(F32)
                ).astype(BF16)
                return carry
            lax.fori_loop(0, 4, add, 0)
        else:
            def add(k, carry):
                h, j = k // 4, k % 4
                part[x, h, j, y] = (
                    part[x, h, j, y].astype(F32) + second[0, h, j].astype(F32) + second[1, h, j].astype(F32)
                ).astype(BF16)
                return carry
            lax.fori_loop(0, 8, add, 0)
        self.local.start()
        for item in self.third:
            item.start()

    def finish(self):
        self.local.wait()
        for item in self.third:
            item.wait_recv()
        third, out = self.third_buf, self.out
        if self.kind == "row":
            out[...] = (
                third[0].astype(F32) + third[1].astype(F32) + third[2].astype(F32) + third[3].astype(F32)
            )
        else:
            for h in range(NC):
                out[h] = (
                    third[0, h].astype(F32) + third[1, h].astype(F32)
                    + third[2, h].astype(F32) + third[3, h].astype(F32)
                )
        for item in self.first + self.second + self.third:
            item.wait_send()


class Home:
    def __init__(self, own, dst, sems):
        x, c, z, y = place()
        self.relay = c == z // 2
        base = sems.used
        for _ in range(2 * NZ + 3):
            sems.take()
        self.go = []
        for dz in range(1, NZ):
            zt = (z + dz) % NZ
            self.go.append(
                pltpu.make_async_remote_copy(
                    src_ref=own.at[zt],
                    dst_ref=dst.at[z % 2],
                    send_sem=sems.ref.at[base + dz],
                    recv_sem=sems.ref.at[base + NZ + z % 2],
                    device_id=(x, c, zt, y),
                    device_id_type=MESH_ID,
                )
            )
        self.stay = pltpu.make_async_copy(own.at[z], dst.at[z % 2], sems.ref.at[base])
        self.arrive = []
        for i in range(2):
            self.arrive.append(
                pltpu.make_async_remote_copy(
                    src_ref=own.at[0],
                    dst_ref=dst.at[i],
                    send_sem=sems.ref.at[base + 1],
                    recv_sem=sems.ref.at[base + NZ + i],
                    device_id=(x, c, z, 1 - y),
                    device_id_type=MESH_ID,
                )
            )

    def start(self):
        @pl.when(self.relay)
        def _():
            self.stay.start()
            for item in self.go:
                item.start()

    def finish(self):
        x, c, z, y = place()

        @pl.when(self.relay)
        def _():
            self.stay.wait()
            for item in self.go:
                item.wait_send()

        for i in range(2):
            @pl.when(2 * c + i != z)
            def _():
                self.arrive[i].wait_recv()


KINDS = ("col", "col", "row", "row", "row")
PART_SHAPES = (
    (2, 2, 4, 2, 24, 1152), (2, 2, 4, 2, 24, 1536), (2, 4, 2, 24, 768), (2, 4, 2, 96, 768), (2, 4, 2, 8, 128),
)


def reduce_buffers(kind, shape):
    block = shape[-2:]
    if kind == "row":
        return [(2, 2) + block, (2, 4) + block, (4,) + block]
    return [(2, 4) + block, (2, 2, 4) + block, (4, 2) + block]


def owner_shape(kind, shape):
    return shape[-2:] if kind == "row" else (2,) + shape[-2:]


def reduce_kernel(kinds, *refs):
    count = len(kinds)
    parts = refs[:count]
    out_rows, back_rows = refs[count:count + 2]
    outs = refs[count + 2:2 * count + 2]
    out_home, back_home = refs[2 * count + 2:2 * count + 4]
    buffers = refs[2 * count + 4:-1]
    sems = Sems(refs[-1])
    items = [
        Reduce(kinds[k], parts[k], sems, *buffers[3 * k:3 * k + 3], outs[k]) for k in range(count)
    ]
    homes = [Home(back_rows, back_home, sems), Home(out_rows, out_home, sems)]
    enter_barrier()
    for item in items:
        item.start_first()
    for home in homes:
        home.start()
    for step in range(count + 1):
        if step < count:
            items[step].start_second()
        if step >= 1:
            items[step - 1].start_third()
    for item in items:
        item.finish()
    for home in homes:
        home.finish()


def reduce_all(kinds, parts, out_rows, back_rows):
    vmem = pl.BlockSpec(memory_space=pltpu.VMEM)
    hbm = pl.BlockSpec(memory_space=pl.ANY)
    count = len(kinds)
    scratch = []
    for kind, part in zip(kinds, parts):
        for shape in reduce_buffers(kind, part.shape):
            scratch.append(pltpu.VMEM(shape, BF16))
    scratch.append(pltpu.SemaphoreType.DMA((GATHER_SEMS,)))
    out_shape = [jax.ShapeDtypeStruct(owner_shape(k, p.shape), F32) for k, p in zip(kinds, parts)]
    out_shape += [jax.ShapeDtypeStruct((2, 128, 768), BF16)] * 2
    return pl.pallas_call(
        partial(reduce_kernel, kinds),
        out_shape=out_shape,
        in_specs=[vmem] * count + [hbm] * 2,
        out_specs=[vmem] * count + [hbm] * 2,
        scratch_shapes=scratch,
        compiler_params=pltpu.CompilerParams(
            collective_id=1, has_side_effects=True, vmem_limit_bytes=60 * 1024 * 1024
        ),
        name="reduce_all",
    )(*parts, out_rows, back_rows)


def swap(value, axis):
    return lax.ppermute(value, axis, [(0, 1), (1, 0)])


def core_sum(value):
    mine = value.astype(BF16)
    other = swap(mine, "c")
    return mine.astype(F32) + other.astype(F32)


def layer_forward(hidden, inputs, weights, key_mask):
    qkv, w_in, w_out, w_down, params = weights
    b_query, b_value, b_in, b_out, b_down, gain_one, shift_one, gain_two, shift_two = params
    rows = hidden.shape[0]
    query = (dot_plain(inputs[:rows], qkv[:, :384]) + b_query).astype(BF16)
    key = dot_plain(inputs, qkv[:, 384:768]).astype(BF16)
    value = (dot_plain(inputs, qkv[:, 768:]) + b_value).astype(BF16)
    q3, k3, v3 = (t.reshape(-1, 6, 64).transpose(1, 0, 2) for t in (query, key, value))
    scores = jnp.einsum("hqd,hkd->hqk", q3, k3, preferred_element_type=F32) * 0.125
    scores = jnp.where(key_mask[None, None, :], scores, NEG)
    log_norm = jax.nn.logsumexp(scores, axis=-1, keepdims=True)
    probs = jnp.exp(scores - log_norm).astype(BF16)
    context = jnp.einsum("hqk,hkd->qhd", probs, v3, preferred_element_type=F32).astype(BF16).reshape(rows, 384)
    first = hidden + core_sum(dot_plain(context, w_out)) + b_out
    normed_one, hat_one, spread_one = layer_norm(first, gain_one, shift_one)
    ff_in = normed_one.astype(BF16)
    pre_act = dot_plain(ff_in, w_in) + b_in
    activated = jax.nn.gelu(pre_act, approximate=False).astype(BF16)
    second = normed_one + core_sum(dot_plain(activated, w_down)) + b_down
    result, hat_two, spread_two = layer_norm(second, gain_two, shift_two)
    kept = (inputs, q3, k3, v3, log_norm, context, hat_one, spread_one, ff_in, pre_act, activated, hat_two, spread_two)
    return result, kept


def layer_backward(back, kept, weights, key_mask):
    qkv, w_in, w_out, w_down, params = weights
    b_query, b_value, b_in, b_out, b_down, gain_one, shift_one, gain_two, shift_two = params
    inputs, q3, k3, v3, log_norm, context, hat_one, spread_one, ff_in, pre_act, activated, hat_two, spread_two = kept
    rows = back.shape[0]
    back_second, g_gain_two, g_shift_two = norm_back(back, hat_two, spread_two, gain_two)
    back_down = back_second.astype(BF16)
    g_down = dot_left_t(activated, back_down)
    g_b_down = jnp.sum(back_down.astype(F32), 0)
    back_act = dot_right_t(back_down, w_down)
    gelu_pull = jax.vjp(partial(jax.nn.gelu, approximate=False), pre_act)[1]
    back_pre = gelu_pull(back_act)[0].astype(BF16)
    g_in = dot_left_t(ff_in, back_pre)
    g_b_in = jnp.sum(back_pre.astype(F32), 0)
    back_normed = back_second + core_sum(dot_right_t(back_pre, w_in))
    back_first, g_gain_one, g_shift_one = norm_back(back_normed, hat_one, spread_one, gain_one)
    back_branch = back_first.astype(BF16)
    g_out = dot_left_t(context, back_branch)
    g_b_out = jnp.sum(back_branch.astype(F32), 0)
    back_context = dot_right_t(back_branch, w_out).astype(BF16)
    b3 = back_context.reshape(rows, 6, 64).transpose(1, 0, 2)
    scores = jnp.einsum("hqd,hkd->hqk", q3, k3, preferred_element_type=F32) * 0.125
    scores = jnp.where(key_mask[None, None, :], scores, NEG)
    probs = jnp.exp(scores - log_norm)
    slope = jnp.einsum("hqd,hkd->hqk", b3, v3, preferred_element_type=F32)
    delta = jnp.sum(probs * slope, -1, keepdims=True)
    score_back = (probs * (slope - delta)).astype(BF16)
    back_value = jnp.einsum("hqk,hqd->khd", probs.astype(BF16), b3, preferred_element_type=F32)
    back_query = jnp.einsum("hqk,hkd->qhd", score_back, k3, preferred_element_type=F32) * 0.125
    back_key = jnp.einsum("hqk,hqd->khd", score_back, q3, preferred_element_type=F32) * 0.125
    back_query = back_query.astype(BF16).reshape(rows, 384)
    back_key = back_key.astype(BF16).reshape(2 * rows, 384)
    back_value = back_value.astype(BF16).reshape(2 * rows, 384)
    g_qkv = jnp.concatenate(
        [dot_left_t(inputs[:rows], back_query), dot_left_t(inputs, back_key), dot_left_t(inputs, back_value)], 1
    )
    g_b_query = jnp.sum(back_query.astype(F32), 0)
    g_b_value = jnp.sum(back_value.astype(F32), 0)
    both = dot_right_t(back_key, qkv[:, 384:768]) + dot_right_t(back_value, qkv[:, 768:])
    mine = both[:rows] + dot_right_t(back_query, qkv[:, :384])
    other = core_sum(both[rows:]).astype(BF16)
    result = back_first + core_sum(mine) + swap(other, "y").astype(F32)
    grads = (g_qkv, g_in, g_out, g_down)
    small = (g_b_query, g_b_value, g_b_in, g_b_out, g_b_down, g_gain_one, g_shift_one, g_gain_two, g_shift_two)
    return result, grads, small


def pick_core(value, core, width):
    both = value.reshape(2, 2, 4 * 2 * width)
    return lax.dynamic_index_in_dim(both, core, 1, keepdims=False).reshape(2, 4, 2, width)


def chip_device(tokens, lengths, slot_sequence, cotangent, w_query, w_key, w_value, w_out, w_in, w_down,
                b_query, b_value, b_out, b_in, b_down, norm1_gain, norm1_bias, norm2_gain, norm2_bias):
    x, c, z, y = place()
    slot = 4 * x + z
    sequence = jnp.sum(jnp.where(lax.iota(jnp.int32, 8) == slot, slot_sequence, 0))
    length = jnp.sum(jnp.where(lax.iota(jnp.int32, 8) == sequence, lengths, 0))
    ids = lax.iota(jnp.int32, 512)
    spot = 256 * (ids // 128) + ids % 128
    own_pos, other_pos = spot + 128 * y, spot + 128 * (1 - y)
    key_mask = jnp.concatenate([own_pos, other_pos]) < length
    row_valid = (own_pos < length)[:, None]

    qkv = jnp.stack([w_query, w_key, w_value]).reshape(3, 2, 24, 2, 2, 192)
    qkv = qkv.transpose(1, 4, 2, 0, 3, 5).reshape(2, 2, 24, 1152)
    win = w_in.reshape(2, 24, 2, 2, 768).transpose(0, 3, 1, 2, 4).reshape(2, 2, 24, 1536)
    small = jnp.concatenate(
        [b_query, b_value, b_out, b_down, norm1_gain, norm1_bias, norm2_gain, norm2_bias, b_in,
         jnp.zeros((2, 224), BF16)], 1).reshape(8, 128)
    (qkv0, qkv1, in0, in1, out0, out1, down0, down1, smalls, own, other, back) = gather_all(
        qkv, win, w_out, w_down, small, tokens, cotangent)
    table = smalls.reshape(32, 2, 512)[:, :, :288].astype(F32)
    wide = table[:, :, :192].reshape(32, 2, 8, 24).transpose(1, 2, 0, 3).reshape(2, 8, 768)
    tall = table[:, :, 192:].transpose(1, 0, 2).reshape(2, 3072)

    def half(vector, width):
        return lax.dynamic_index_in_dim(vector.reshape(2, 2, width), c, 1, keepdims=False).reshape(2 * width)

    weights = []
    for layer, group in enumerate(((qkv0, in0, out0, down0), (qkv1, in1, out1, down1))):
        bq, bv, bo, bd, g1, s1, g2, s2 = (wide[layer, k] for k in range(8))
        params = (half(bq, 192), half(bv, 192), half(tall[layer], 768), bo, bd, g1, s1, g2, s2)
        weights.append((group[0].reshape(768, 1152), group[1].reshape(768, 1536),
                        group[2].reshape(384, 768), group[3].reshape(1536, 768), params))

    own = own.reshape(512, 768)
    other = other.reshape(512, 768)
    hidden = own.astype(F32)
    inputs = jnp.concatenate([own, other], 0)
    kept = []
    for layer in range(2):
        hidden, saved = layer_forward(hidden, inputs, weights[layer], key_mask)
        kept.append(saved)
        if layer == 0:
            mine = hidden.astype(BF16)
            inputs = jnp.concatenate([mine, swap(mine, "y")], 0)
    back = jnp.where(row_valid, back.reshape(512, 768).astype(F32), 0.0)
    parts, smalls = [None] * 2, [None] * 2
    for layer in (1, 0):
        back, grads, small = layer_backward(back, kept[layer], weights[layer], key_mask)
        g_qkv, g_in, g_out, g_down = grads
        parts[layer] = [g_qkv.astype(BF16).reshape(PART_SHAPES[0]), g_in.astype(BF16).reshape(PART_SHAPES[1]),
                        g_out.astype(BF16).reshape(PART_SHAPES[2]), g_down.astype(BF16).reshape(PART_SHAPES[3])]
        bq, bv, bi, bo, bd, g1, s1, g2, s2 = small
        pieces = [bq.reshape(2, 4, 2, 24), bv.reshape(2, 4, 2, 24)]
        pieces += [pick_core(v, c, 24) for v in (bo, bd, g1, s1, g2, s2)]
        pieces += [bi.reshape(2, 4, 2, 96), jnp.zeros((2, 4, 2, 224), F32)]
        smalls[layer] = jnp.concatenate(pieces, -1)
    small_part = jnp.concatenate(smalls, -1).reshape(2, 4, 2, 8, 128).astype(BF16)
    kinds = KINDS[:4] + KINDS
    out = reduce_all(kinds, parts[1] + parts[0] + [small_part],
                     hidden.astype(BF16).reshape(4, 128, 768), back.astype(BF16).reshape(4, 128, 768))
    qkv_out = jnp.stack([out[4], out[0]]).reshape(2, 2, 24, 3, 2, 192)
    qkv_out = qkv_out.transpose(3, 0, 2, 4, 1, 5).reshape(3, 2, 24, 768)
    in_out = jnp.stack([out[5], out[1]]).reshape(2, 2, 24, 2, 768).transpose(0, 2, 3, 1, 4).reshape(2, 24, 3072)
    vec = out[8].reshape(2, 512)
    vecs = [vec[:, 24 * k:24 * k + 24] for k in range(8)]
    return (out[9].astype(F32), out[10].astype(F32), qkv_out[0], qkv_out[1], qkv_out[2],
            jnp.stack([out[6], out[2]]), in_out, jnp.stack([out[7], out[3]]),
            vecs[0], vecs[1], vecs[2], vec[:, 192:288], vecs[3], vecs[4], vecs[5], vecs[6], vecs[7])


def solution(mesh):
    if dict(mesh.shape) != {"head": 4, "blk": 8}:
        return plain_solution(mesh)
    grid = Mesh(mesh.devices.reshape(NX, NC, NZ, NY), AXES)
    rows = P(("x", "c"), ("z", "y"), None)
    wide = P(None, AXES, None)
    flat = P(None, AXES)
    return jax.shard_map(
        chip_device,
        mesh=grid,
        in_specs=(rows, P(), P(), rows) + (wide,) * 6 + (flat,) * 9,
        out_specs=(rows, rows) + (wide,) * 6 + (flat,) * 9,
        check_vma=False,
    )
```
